32 devices in a mesh: row: 8 (over z, x), col: 4 (over y, core).
Axes of the slice: x: 2, y: 2, z: 4, core: 2. Of those that a mesh axis runs over, the one named last changes fastest.
Arguments:
- x_first: bfloat16 [768, 18432], P(None, ('row', 'col')), may hold values from -1.5 to 1.5
- x_second: bfloat16 [768, 18432], P(None, ('row', 'col')), may hold values from -1.5 to 1.5
- w_first: bfloat16 [18432, 256], P(('row', 'col')), may hold values from -12 to 12
- w_second: bfloat16 [18432, 256], P(('row', 'col')), may hold values from -12 to 12
- counts: int32 [2], replicated, may hold values from 384 to 768
- damping: float32 [1], replicated, may hold values from 0.2 to 0.6
- eig_low: float32 [1], replicated, may hold values from 0.1 to 0.4
- eig_high: float32 [1], replicated, may hold values from 3 to 6
Outputs:
- merged: float32 [18432, 256], P(('row', 'col'))
- residual: float32 [18432, 256], P(('row', 'col'))
The draws below stay inside these ranges and needn't reach their ends.
Inputs may be any that keep to these rules, and one draw needn't show every extreme that they name: counts[i] is how many leading rows of domain i are used; later rows are ignored.
All inputs are finite; a program needn't handle non-finite values.
Results may differ from the reference program's by a relative error of at most 0.0003.
Values may be sent and summed in bfloat16 or wider, within the bound.
A program may use at most 64 MiB of HBM per device.

```python
import jax
import jax.numpy as jnp
from jax import lax

D = 18432
ROWS = 768
COLS = 256
ITERS = 2


def shard_levels(own_key, shape, shards, smallest, high):
    level, own = 1.0, jax.random.fold_in(own_key, 6)
    for axis_at, blocks in shards:
        heights = jnp.exp(jax.random.uniform(jax.random.fold_in(own, axis_at), (blocks,), jnp.float32, smallest / len(shards), high / len(shards)))
        level = level * jnp.repeat(heights, shape[axis_at] // blocks).reshape([-1 if axis == axis_at else 1 for axis in range(len(shape))])
    return level


def bell_draw(stream_key, dims, deviation, reach, pieces=(), kind=jnp.bfloat16):
    result = jax.random.normal(stream_key, dims, jnp.float32) * deviation
    if len(pieces) > 0:
        result = shard_levels(stream_key, dims, pieces, -0.22, 0.18) * result
    return jnp.clip(result, min=-reach, max=reach).astype(kind)


def setup_inputs(seed: int = 0) -> dict:
    keys = jax.random.split(jax.random.key(seed), 9)
    x_first = bell_draw(keys[0], (ROWS, D), 0.25, 1.5, ((1, 32),))
    x_second = bell_draw(keys[1], (ROWS, D), 0.25, 1.5, ((1, 32),))
    w_first = bell_draw(keys[2], (D, COLS), 2.0, 12.0, ((0, 32),))
    w_second = bell_draw(keys[3], (D, COLS), 2.0, 12.0, ((0, 32),))
    counts = jax.random.randint(keys[4], (2,), ROWS // 2, ROWS + 1).astype(jnp.int32)
    damping = jnp.clip(jax.random.uniform(keys[5], (1,), jnp.float32, 0.2, 0.6), 0.2, 0.6)
    eig_low = jnp.clip(jax.random.uniform(keys[6], (1,), jnp.float32, 0.1, 0.4), 0.1, 0.4)
    eig_high = jnp.clip(jax.random.uniform(keys[7], (1,), jnp.float32, 3.0, 6.0), 3.0, 6.0)
    return {"x_first": x_first, "x_second": x_second, "w_first": w_first, "w_second": w_second, "counts": counts, "damping": damping, "eig_low": eig_low, "eig_high": eig_high}


def gram_apply(dense, scale, vector):
    inner = jnp.dot(dense, vector, precision=lax.Precision.HIGHEST, preferred_element_type=jnp.float32)
    return jnp.dot(dense.T, inner, precision=lax.Precision.HIGHEST, preferred_element_type=jnp.float32) * scale


def reference(x_first, x_second, w_first, w_second, counts, damping, eig_low, eig_high):
    position = jnp.arange(x_first.shape[0], dtype=jnp.int32)
    dense_first = x_first.astype(jnp.float32) * (position < counts[0]).astype(jnp.float32)[:, None]
    dense_second = x_second.astype(jnp.float32) * (position < counts[1]).astype(jnp.float32)[:, None]
    scale_first = 1.0 / counts[0].astype(jnp.float32)
    scale_second = 1.0 / counts[1].astype(jnp.float32)
    ridge = damping[0]
    rhs = gram_apply(dense_first, scale_first, w_first.astype(jnp.float32)) + gram_apply(dense_second, scale_second, w_second.astype(jnp.float32))
    middle = (eig_high[0] + eig_low[0]) / 2.0
    radius = (eig_high[0] - eig_low[0]) / 2.0
    sigma = middle / radius
    rho_now = 1.0 / sigma
    merged = jnp.zeros_like(rhs)
    residual = rhs
    direction = rhs / middle
    for step_index in range(ITERS):
        image = gram_apply(dense_first, scale_first, direction) + gram_apply(dense_second, scale_second, direction) + ridge * direction
        merged = merged + direction
        residual = residual - image
        rho_new = 1.0 / (2.0 * sigma - rho_now)
        direction = rho_new * rho_now * direction + (2.0 * rho_new / radius) * residual
        rho_now = rho_new
    return merged, residual
```

```python
import functools

import jax
import jax.numpy as jnp
from jax import lax
from jax.experimental import pallas as pl
from jax.experimental.pallas import tpu as pltpu
from jax.sharding import PartitionSpec as P

ITERS = 2
HALVES = 2
LANES = 128
SUBLANES = 8
REDUCTIONS = ITERS + 1


def axis_groups(name, size):
    pair = 2 if size % 2 == 0 else 1
    found = [(name, 1, pair), (name, pair, size // pair)]
    return [group for group in found if group[2] > 1]


def plan(mesh_shape, rows):
    col = axis_groups("col", mesh_shape["col"])
    row = axis_groups("row", mesh_shape["row"])
    orders = [col[:1] + row[:1] + col[1:] + row[1:], col[:1] + col[1:] + row[:1] + row[1:]]
    result = []
    for order in orders:
        height, stages = rows, []
        for group in order:
            members = group[2]
            split = height % (members * SUBLANES) == 0
            chunk = height // members if split else height
            stages.append((group, height, chunk, split))
            height = chunk
        result.append(stages)
    return result


def member_of(group):
    name, stride, members = group
    return lax.rem(lax.div(lax.axis_index(name), stride), members)


def peer_at(group, offset):
    name, stride, members = group
    me = member_of(group)
    other = lax.rem(me + offset, members)
    return {name: lax.axis_index(name) + (other - me) * stride}, other


def kernel(
    stages_of, groups, counts, damping, eig_low, eig_high, x_first, x_second, w_first, w_second,
    merged, residual, dense, sums, full, d_zero, rest, high, low, q_high, q_low, *more,
):
    landing = more[: len(stages_of)]
    send_sem, recv_sem = more[len(stages_of) :]
    rows = x_first.shape[0]
    per_part = [sum(group[2] - 1 for group, _, _, _ in stages) for stages in stages_of]
    most = max(per_part)

    barrier = pltpu.get_barrier_semaphore()
    partners = 0
    for group in groups:
        for offset in range(1, group[2]):
            pl.semaphore_signal(
                barrier, inc=1, device_id=peer_at(group, offset)[0], device_id_type=pl.DeviceIdType.MESH
            )
            partners += 1

    def lane(value):
        return jnp.full((1, LANES), value, jnp.float32)

    scales = [1.0 / lane(counts[i].astype(jnp.float32)) for i in range(2)]
    ridge = lane(damping[0])
    middle = (lane(eig_high[0]) + lane(eig_low[0])) / 2.0
    radius = (lane(eig_high[0]) - lane(eig_low[0])) / 2.0
    sigma = middle / radius

    position = lax.broadcasted_iota(jnp.int32, x_first.shape, 0)
    for domain, source in enumerate((x_first, x_second)):
        value = source[...].astype(jnp.float32)
        dense[pl.ds(domain * rows, rows), :] = jnp.where(position < counts[domain], value, 0.0).astype(jnp.bfloat16)

    def reduce_all(index, produce):
        sent = []
        parts = [(domain, half) for domain in range(2) for half in range(HALVES)]

        def start(part, phase, slot, src, dst, device):
            at = (index * 2 + phase, part, slot)
            copy = pltpu.make_async_remote_copy(
                src_ref=src, dst_ref=dst, send_sem=send_sem.at[at], recv_sem=recv_sem.at[at],
                device_id=device, device_id_type=pl.DeviceIdType.MESH,
            )
            copy.start()
            return copy

        state = {}

        def launch_scatter(part, stage):
            domain, half = parts[part]
            group, height, chunk, split = stages_of[half][stage]
            base = state[part]["base"]
            slot0 = state[part]["slot"]
            copies = []
            for offset in range(1, group[2]):
                device, other = peer_at(group, offset)
                begin = base + other * chunk if split else base
                begin = pl.multiple_of(begin, SUBLANES)
                spot = state[part]["spot"] + (offset - 1) * chunk
                copies.append(
                    start(
                        part, 0, slot0 + offset - 1,
                        sums.at[half, pl.ds(domain * rows + begin, chunk), :],
                        landing[half].at[index, domain, pl.ds(spot, chunk), :],
                        device,
                    )
                )
            if split:
                sent.extend(copies)
            state[part]["wait"] = copies

        def finish_scatter(part, stage):
            domain, half = parts[part]
            group, height, chunk, split = stages_of[half][stage]
            st = state[part]
            st["bases"].append(st["base"])
            if split:
                st["base"] = st["base"] + member_of(group) * chunk
            own = pl.ds(pl.multiple_of(domain * rows + st["base"], SUBLANES), chunk)
            last = stage == len(stages_of[half]) - 1
            if not split:
                for copy in st["wait"]:
                    copy.wait_send()
            for copy in st["wait"]:
                copy.wait_recv()
            total = sums[half, own, :]
            for offset in range(1, group[2]):
                total = total + landing[half][index, domain, pl.ds(st["spot"] + (offset - 1) * chunk, chunk), :]
            if last:
                full[index, half, own, :] = total
            else:
                sums[half, own, :] = total
            st["spot"] += (group[2] - 1) * chunk
            st["slot"] += group[2] - 1

        def launch_gather(part, stage):
            domain, half = parts[part]
            group, height, chunk, split = stages_of[half][stage]
            st = state[part]
            st["slot"] -= group[2] - 1
            copies = []
            if split:
                begin = pl.multiple_of(domain * rows + st["base"], SUBLANES)
                for offset in range(1, group[2]):
                    where = full.at[index, half, pl.ds(begin, chunk), :]
                    device, _ = peer_at(group, offset)
                    copies.append(start(part, 1, st["slot"] + offset - 1, where, where, device))
            st["base"] = st["bases"].pop()
            sent.extend(copies)
            st["wait"] = copies

        def finish_gather(part):
            for copy in state[part]["wait"]:
                copy.wait_recv()

        count = [len(stages_of[half]) for _, half in parts]
        for domain in range(2):
            produce(domain)
            if index == 0 and domain == 0:
                pl.semaphore_wait(barrier, partners)
            for half in range(HALVES):
                part = domain * HALVES + half
                state[part] = {"base": 0, "slot": 0, "spot": 0, "bases": []}
                launch_scatter(part, 0)
        for stage in range(max(count)):
            for part in range(len(parts)):
                if stage < count[part]:
                    finish_scatter(part, stage)
                    if stage + 1 < count[part]:
                        launch_scatter(part, stage + 1)
                    else:
                        launch_gather(part, stage)
        for stage in reversed(range(max(count))):
            for part in range(len(parts)):
                if stage < count[part]:
                    finish_gather(part)
                    if stage > 0:
                        launch_gather(part, stage - 1)
        return sent

    def settle(sent):
        for copy in sent:
            copy.wait_send()

    def split_store(domain, half, value):
        place = pl.ds(domain * rows, rows), pl.ds(half * LANES, LANES)
        top = value.astype(jnp.bfloat16)
        high[place] = top
        low[place] = (value - top.astype(jnp.float32)).astype(jnp.bfloat16)

    def back_project():
        contract = (((0,), (0,)), ((), ()))
        return lax.dot_general(
            dense[...], high[...], contract, preferred_element_type=jnp.float32
        ) + lax.dot_general(dense[...], low[...], contract, preferred_element_type=jnp.float32)

    def store_sums(domain, value):
        for half in range(HALVES):
            sums[half, pl.ds(domain * rows, rows), :] = value[:, half * LANES : (half + 1) * LANES]

    def first_product(domain):
        weights = (w_first, w_second)[domain]
        store_sums(
            domain,
            jnp.dot(dense[pl.ds(domain * rows, rows), :], weights[...], preferred_element_type=jnp.float32),
        )

    def next_product(domain):
        part = dense[pl.ds(domain * rows, rows), :]
        store_sums(
            domain,
            jnp.dot(part, q_high[...], preferred_element_type=jnp.float32)
            + jnp.dot(part, q_low[...], preferred_element_type=jnp.float32),
        )

    def project_and_sum(index):
        seen = back_project()
        top = seen.astype(jnp.bfloat16)
        q_high[...] = top
        q_low[...] = (seen - top.astype(jnp.float32)).astype(jnp.bfloat16)
        if index == 1:
            merged[...] = seen
        else:
            merged[...] = merged[...] + seen
        return reduce_all(index, next_product)

    sent = reduce_all(0, first_product)
    settle(sent)
    blocks = [(domain, half, pl.ds(domain * rows, rows)) for domain in range(2) for half in range(HALVES)]
    for domain, half, place in blocks:
        value = full[0, half, place, :] * scales[domain]
        rest[half, place, :] = value
        value = value / middle
        d_zero[half, place, :] = value
        split_store(domain, half, value)
    rho_now = 1.0 / sigma
    for step in range(ITERS):
        settle(project_and_sum(step + 1))
        rho_new = 1.0 / (2.0 * sigma - rho_now)
        for domain, half, place in blocks:
            direction = d_zero[half, place, :]
            left = rest[half, place, :] - (full[step + 1, half, place, :] * scales[domain] + ridge * direction)
            if step + 1 < ITERS:
                rest[half, place, :] = left
                direction = rho_new * rho_now * direction + (2.0 * rho_new / radius) * left
                d_zero[half, place, :] = direction
                split_store(domain, half, direction)
            else:
                split_store(domain, half, left)
        rho_now = rho_new
    residual[...] = back_project()


def solution(mesh):
    shape = dict(mesh.shape)

    def body(x_first, x_second, w_first, w_second, counts, damping, eig_low, eig_high):
        rows, features = x_first.shape
        columns = w_first.shape[1]
        stages_of = plan(shape, rows)
        groups = axis_groups("col", shape["col"]) + axis_groups("row", shape["row"])
        slots = max(sum(stage[0][2] - 1 for stage in stages) for stages in stages_of)
        spots = [sum((stage[0][2] - 1) * stage[2] for stage in stages) for stages in stages_of]
        smem = pl.BlockSpec(memory_space=pltpu.SMEM)
        vmem = pl.BlockSpec(memory_space=pltpu.VMEM)
        out = jax.ShapeDtypeStruct((features, columns), jnp.float32)
        wide = (HALVES, 2 * rows, LANES)
        semaphores = pltpu.SemaphoreType.DMA((REDUCTIONS * 2, 2 * HALVES, slots))
        return pl.pallas_call(
            functools.partial(kernel, stages_of, groups),
            out_shape=(out, out),
            in_specs=[smem] * 4 + [vmem] * 4,
            out_specs=(vmem, vmem),
            scratch_shapes=[
                pltpu.VMEM((2 * rows, features), jnp.bfloat16),
                pltpu.VMEM(wide, jnp.float32),
                pltpu.VMEM((REDUCTIONS,) + wide, jnp.float32),
                pltpu.VMEM(wide, jnp.float32),
                pltpu.VMEM(wide, jnp.float32),
                pltpu.VMEM((2 * rows, columns), jnp.bfloat16),
                pltpu.VMEM((2 * rows, columns), jnp.bfloat16),
                pltpu.VMEM((features, columns), jnp.bfloat16),
                pltpu.VMEM((features, columns), jnp.bfloat16),
            ]
            + [pltpu.VMEM((REDUCTIONS, 2, spot, LANES), jnp.float32) for spot in spots]
            + [semaphores, semaphores],
            compiler_params=pltpu.CompilerParams(
                collective_id=0, has_side_effects=True, vmem_limit_bytes=60 * 1024 * 1024
            ),
        )(counts, damping, eig_low, eig_high, x_first, x_second, w_first, w_second)

    both = ("row", "col")
    return jax.shard_map(
        body,
        mesh=mesh,
        in_specs=(P(None, both), P(None, both), P(both, None), P(both, None), P(), P(), P(), P()),
        out_specs=(P(both, None), P(both, None)),
        check_vma=False,
    )
```

```python
import functools

import jax
import jax.numpy as jnp
from jax import lax
from jax.experimental import pallas as pl
from jax.experimental.pallas import tpu as pltpu
from jax.sharding import PartitionSpec as P

ITERS = 2
HALVES = 2
LANES = 128
SUBLANES = 8
REDUCTIONS = ITERS + 1
LEVELS = 32760.0
TINY = 1e-30


def axis_groups(name, size):
    pair = 2 if size % 2 == 0 else 1
    found = [(name, 1, pair), (name, pair, size // pair)]
    return [group for group in found if group[2] > 1]


def joined(parts):
    members = 1
    for part in parts:
        members *= part[2]
    return [(tuple(parts), None, members)] if members > 1 else []


def plan(mesh_shape, rows):
    col = axis_groups("col", mesh_shape["col"])
    row = axis_groups("row", mesh_shape["row"])
    order = joined(col[:1]) + joined(row[:1] + col[1:]) + joined(row[1:])
    orders = [order] * HALVES
    result = []
    for order in orders:
        height, stages = rows, []
        for group in order:
            members = group[2]
            split = height % (members * SUBLANES) == 0
            chunk = height // members if split else height
            stages.append((group, height, chunk, split))
            height = chunk
        result.append(stages)
    return result


def member_of(group):
    index, weight = 0, 1
    for name, stride, members in group[0]:
        index = index + lax.rem(lax.div(lax.axis_index(name), stride), members) * weight
        weight *= members
    return index


def peer_at(group, offset):
    device, index, weight = {}, 0, 1
    for name, stride, members in group[0]:
        me = lax.rem(lax.div(lax.axis_index(name), stride), members)
        other = lax.rem(me + offset % members, members)
        device[name] = device.get(name, lax.axis_index(name)) + (other - me) * stride
        index = index + other * weight
        offset, weight = offset // members, weight * members
    return device, index


def kernel(
    stages_of, groups, counts, damping, eig_low, eig_high, x_first, x_second, w_first, w_second,
    merged, residual, dense, turned, sums, coded, steps, d_zero, rest, pieces, q_pieces, *more,
):
    depth = max(len(stages) for stages in stages_of)
    outgoing, landing = more[:depth], more[depth : 2 * depth]
    out_steps, in_steps, send_sem, recv_sem = more[2 * depth :]
    rows = x_first.shape[0]
    final = stages_of[0][-1][2]

    barrier = pltpu.get_barrier_semaphore()
    partners = 0
    for group in groups:
        for offset in range(1, group[2]):
            pl.semaphore_signal(
                barrier, inc=1, device_id=peer_at(group, offset)[0], device_id_type=pl.DeviceIdType.MESH
            )
            partners += 1

    def lane(value):
        return jnp.full((1, LANES), value, jnp.float32)

    scales = [1.0 / lane(counts[i].astype(jnp.float32)) for i in range(2)]
    ridge = lane(damping[0])
    middle = (lane(eig_high[0]) + lane(eig_low[0])) / 2.0
    radius = (lane(eig_high[0]) - lane(eig_low[0])) / 2.0
    sigma = middle / radius

    position = lax.broadcasted_iota(jnp.int32, x_first.shape, 0)
    for domain, source in enumerate((x_first, x_second)):
        value = source[...].astype(jnp.float32)
        dense[pl.ds(domain * rows, rows), :] = jnp.where(position < counts[domain], value, 0.0).astype(jnp.bfloat16)

    def reduce_all(index, produce):
        sent = []
        parts = [(domain, half) for domain in range(2) for half in range(HALVES)]

        def start(part, slot, src, dst, device):
            at = (index, part, slot)
            copy = pltpu.make_async_remote_copy(
                src_ref=src, dst_ref=dst, send_sem=send_sem.at[at], recv_sem=recv_sem.at[at],
                device_id=device, device_id_type=pl.DeviceIdType.MESH,
            )
            copy.start()
            return copy

        state = {}

        def launch_scatter(part, stage):
            domain, half = parts[part]
            group, height, chunk, split = stages_of[half][stage]
            base = state[part]["base"]
            copies = []
            for offset in range(1, group[2]):
                device, other = peer_at(group, offset)
                begin = domain * rows + base + (other * chunk if split else 0)
                slot = state[part]["slot"] + offset - 1
                value = sums[half, pl.ds(pl.multiple_of(begin, SUBLANES), chunk), :]
                outgoing[stage][part, offset - 1, pl.ds(0, chunk), :], out_steps[part, slot] = fixed(value)
                held, room = outgoing[stage], landing[stage]
                copies.append(
                    start(
                        part, slot,
                        held.at[part, offset - 1, pl.ds(0, chunk), :],
                        room.at[index, part, offset - 1, pl.ds(0, chunk), :],
                        device,
                    )
                )
                copies.append(
                    start(len(parts) + part, slot, out_steps.at[part, slot], in_steps.at[index, part, slot], device)
                )
            sent.extend(copies)
            state[part]["wait"] = copies

        def finish_scatter(part, stage):
            domain, half = parts[part]
            group, height, chunk, split = stages_of[half][stage]
            st = state[part]
            st["bases"].append(st["base"])
            if split:
                st["base"] = st["base"] + member_of(group) * chunk
            own = pl.ds(pl.multiple_of(domain * rows + st["base"], SUBLANES), chunk)
            for copy in st["wait"]:
                copy.wait_recv()
            total = sums[half, own, :]
            for offset in range(1, group[2]):
                sent_here = landing[stage][index, part, offset - 1, pl.ds(0, chunk), :]
                total = total + sent_here.astype(jnp.int32).astype(jnp.float32) * in_steps[index, part, st["slot"] + offset - 1]
            if stage == len(stages_of[half]) - 1:
                st["total"] = total
            else:
                sums[half, own, :] = total
            st["slot"] += group[2] - 1

        def fixed(value):
            top = jnp.maximum(jnp.max(jnp.abs(value), axis=0, keepdims=True), TINY)
            return jnp.round(value * (LEVELS / top)).astype(jnp.int32).astype(jnp.int16), top * (1.0 / LEVELS)

        def encode(half):
            pair = jnp.concatenate([state[half]["total"], state[HALVES + half]["total"]], axis=0)
            mine = lax.div(state[half]["base"], final)
            coded[index, half, mine], steps[index, half, mine] = fixed(pair)

        def launch_gather(half, stage):
            group, height, chunk, split = stages_of[half][stage]
            st = state[half]
            st["slot"] -= group[2] - 1
            copies = []
            if split:
                where = pl.ds(lax.div(st["base"], final), chunk // final)
                for offset in range(1, group[2]):
                    device, _ = peer_at(group, offset)
                    slot = st["slot"] + offset - 1
                    for phase, held in ((0, coded), (1, steps)):
                        place = held.at[index, half, where]
                        copies.append(start(2 * len(parts) + 2 * half + phase, slot, place, place, device))
            st["base"] = st["bases"].pop()
            sent.extend(copies)
            st["wait"] = copies

        def finish_gather(half):
            for copy in state[half]["wait"]:
                copy.wait_recv()

        count = [len(stages_of[half]) for _, half in parts]
        for domain in range(2):
            produce(domain)
            if index == 0 and domain == 0:
                pl.semaphore_wait(barrier, partners)
            for half in range(HALVES):
                part = domain * HALVES + half
                state[part] = {"base": 0, "slot": 0, "bases": []}
                launch_scatter(part, 0)
        if index == 0:
            turned[...] = dense[...].T
        for stage in range(max(count)):
            for part in range(len(parts)):
                if stage < count[part]:
                    finish_scatter(part, stage)
                    if stage + 1 < count[part]:
                        launch_scatter(part, stage + 1)
                    elif part >= HALVES:
                        encode(part - HALVES)
                        launch_gather(part - HALVES, stage)
        for stage in reversed(range(max(count))):
            for half in range(HALVES):
                if stage < count[half]:
                    finish_gather(half)
                    if stage > 0:
                        launch_gather(half, stage - 1)
        return sent

    def summed(index, domain, half):
        value = coded[index, half].astype(jnp.int32).astype(jnp.float32) * steps[index, half]
        return value[:, domain * final : (domain + 1) * final, :].reshape(rows, LANES)

    def settle(sent):
        for copy in sent:
            copy.wait_send()

    def split_store(domain, half, value):
        place = pl.ds(domain * rows, rows)
        top = value.astype(jnp.bfloat16)
        pieces[place, pl.ds(half * LANES, LANES)] = top
        pieces[place, pl.ds((HALVES + half) * LANES, LANES)] = (value - top.astype(jnp.float32)).astype(jnp.bfloat16)

    def back_project():
        both = jnp.dot(turned[...], pieces[...], preferred_element_type=jnp.float32)
        return both[:, : HALVES * LANES] + both[:, HALVES * LANES :]

    def store_sums(domain, value):
        for half in range(HALVES):
            sums[half, pl.ds(domain * rows, rows), :] = value[:, half * LANES : (half + 1) * LANES]

    def first_product(domain):
        weights = (w_first, w_second)[domain]
        store_sums(
            domain,
            jnp.dot(dense[pl.ds(domain * rows, rows), :], weights[...], preferred_element_type=jnp.float32),
        )

    def next_product(domain):
        both = jnp.dot(dense[pl.ds(domain * rows, rows), :], q_pieces[...], preferred_element_type=jnp.float32)
        store_sums(domain, both[:, : HALVES * LANES] + both[:, HALVES * LANES :])

    def project_and_sum(index):
        seen = back_project()
        top = seen.astype(jnp.bfloat16)
        q_pieces[:, : HALVES * LANES] = top
        q_pieces[:, HALVES * LANES :] = (seen - top.astype(jnp.float32)).astype(jnp.bfloat16)
        if index == 1:
            merged[...] = seen
        else:
            merged[...] = merged[...] + seen
        return reduce_all(index, next_product)

    sent = reduce_all(0, first_product)
    settle(sent)
    blocks = [(domain, half, pl.ds(domain * rows, rows)) for domain in range(2) for half in range(HALVES)]
    for domain, half, place in blocks:
        value = summed(0, domain, half) * scales[domain]
        rest[half, place, :] = value
        value = value / middle
        d_zero[half, place, :] = value
        split_store(domain, half, value)
    rho_now = 1.0 / sigma
    for step in range(ITERS):
        settle(project_and_sum(step + 1))
        rho_new = 1.0 / (2.0 * sigma - rho_now)
        for domain, half, place in blocks:
            direction = d_zero[half, place, :]
            left = rest[half, place, :] - (summed(step + 1, domain, half) * scales[domain] + ridge * direction)
            if step + 1 < ITERS:
                rest[half, place, :] = left
                direction = rho_new * rho_now * direction + (2.0 * rho_new / radius) * left
                d_zero[half, place, :] = direction
                split_store(domain, half, direction)
            else:
                split_store(domain, half, left)
        rho_now = rho_new
    residual[...] = back_project()


def solution(mesh):
    shape = dict(mesh.shape)

    def body(x_first, x_second, w_first, w_second, counts, damping, eig_low, eig_high):
        rows, features = x_first.shape
        columns = w_first.shape[1]
        stages_of = plan(shape, rows)
        groups = [stage[0] for stage in stages_of[0]]
        slots = max(sum(stage[0][2] - 1 for stage in stages) for stages in stages_of)
        levels = [
            (max(stages[at][0][2] for stages in stages_of) - 1, max(stages[at][2] for stages in stages_of), LANES)
            for at in range(len(stages_of[0]))
        ]
        final = stages_of[0][-1][2]
        blocks = rows // final
        smem = pl.BlockSpec(memory_space=pltpu.SMEM)
        vmem = pl.BlockSpec(memory_space=pltpu.VMEM)
        out = jax.ShapeDtypeStruct((features, columns), jnp.float32)
        wide = (HALVES, 2 * rows, LANES)
        semaphores = pltpu.SemaphoreType.DMA((REDUCTIONS, 6 * HALVES, slots))
        return pl.pallas_call(
            functools.partial(kernel, stages_of, groups),
            out_shape=(out, out),
            in_specs=[smem] * 4 + [vmem] * 4,
            out_specs=(vmem, vmem),
            scratch_shapes=[
                pltpu.VMEM((2 * rows, features), jnp.bfloat16),
                pltpu.VMEM((features, 2 * rows), jnp.bfloat16),
                pltpu.VMEM(wide, jnp.float32),
                pltpu.VMEM((REDUCTIONS, HALVES, blocks, 2 * final, LANES), jnp.int16),
                pltpu.VMEM((REDUCTIONS, HALVES, blocks, 1, LANES), jnp.float32),
                pltpu.VMEM(wide, jnp.float32),
                pltpu.VMEM(wide, jnp.float32),
                pltpu.VMEM((2 * rows, 2 * columns), jnp.bfloat16),
                pltpu.VMEM((features, 2 * columns), jnp.bfloat16),
            ]
            + [pltpu.VMEM((2 * HALVES,) + level, jnp.int16) for level in levels]
            + [pltpu.VMEM((REDUCTIONS, 2 * HALVES) + level, jnp.int16) for level in levels]
            + [
                pltpu.VMEM((2 * HALVES, slots, 1, LANES), jnp.float32),
                pltpu.VMEM((REDUCTIONS, 2 * HALVES, slots, 1, LANES), jnp.float32),
            ]
            + [semaphores, semaphores],
            compiler_params=pltpu.CompilerParams(
                collective_id=0, has_side_effects=True, vmem_limit_bytes=60 * 1024 * 1024
            ),
        )(counts, damping, eig_low, eig_high, x_first, x_second, w_first, w_second)

    both = ("row", "col")
    return jax.shard_map(
        body,
        mesh=mesh,
        in_specs=(P(None, both), P(None, both), P(both, None), P(both, None), P(), P(), P(), P()),
        out_specs=(P(both, None), P(both, None)),
        check_vma=False,
    )
```
